512 devices in a mesh: state: 64 (over y_hi, z, x), lat: 8 (over y_lo, core).
Axes of the slice: x: 4, y: 8 (y_hi: 2, y_lo: 4; y = y_hi * 4 + y_lo), z: 8, core: 2. Of those that a mesh axis runs over, the one named last changes fastest.
Arguments:
- spins: int32 [64, 8, 128], P('state', 'lat'), may hold values from -1 to 1, as said below
- embed_w: bfloat16 [64, 9], replicated, may hold values from -2 to 2
- block_w: bfloat16 [16, 1, 2, 64, 576], replicated, may hold values from -0.25 to 0.25
- readout: bfloat16 [16, 64], replicated, may hold values from -0.09375 to 0.09375
- amp_cot: float32 [16, 64], replicated, may hold values from -6 to 6
Outputs:
- log_amp: float32 [16, 64], replicated
- block_grad: float32 [1024, 1, 2, 576], P('state')
- embed_grad: float32 [64, 9], replicated
The draws below stay inside these ranges and needn't reach their ends.
Inputs may be any that keep to these rules, and one draw needn't show every extreme that they name: `spins`: every entry is -1 or +1.
All inputs are finite; a program needn't handle non-finite values.
Results may differ from the reference program's by a relative error of at most 0.00083.
Values may be sent and summed in bfloat16 or wider, within the bound.
No kernel may reach another device: no remote copies, remote signals or barrier semaphores. Data moves between devices by JAX's collectives and lax.ppermute only.
A program may use at most 64 MiB of HBM per device.

```python
import math
import jax
import jax.numpy as jnp
from jax import lax

C = 64
LY = 128
STATES = 16
BLOCKS = 1
WALKERS = 64
LX = 8


def draw_spins(key, part):
    random_bits = jax.random.randint(key, (WALKERS, LX, LY), 0, 2)
    return (2 * random_bits - 1).astype(jnp.int32)


def normal_values(own_key, extent, scale, reach, kind=jnp.bfloat16):
    drawn = jax.random.normal(own_key, extent, jnp.float32) * scale
    return jnp.minimum(jnp.maximum(drawn, -reach), reach).astype(kind)


def setup_inputs(seed: int = 0) -> dict:
    streams_of = jax.random.split(jax.random.key(seed), 6)
    return {
        "spins": draw_spins(jax.random.fold_in(streams_of[5], 71), 0),
        "embed_w": normal_values(streams_of[1], (C, 9), 9 ** -0.5, 2.0),
        "block_w": normal_values(streams_of[2], (STATES, BLOCKS, 2, C, 9 * C), (9 * C) ** -0.5, 0.25),
        "readout": normal_values(streams_of[3], (STATES, C), (C * 64) ** -0.5, 0.09375),
        "amp_cot": normal_values(streams_of[4], (STATES, WALKERS), 1.0, 6.0, jnp.float32),
    }


def conv_field(padded, weight):
    row_count = padded.shape[2] - 2
    col_count = padded.shape[3] - 2
    out_count = weight.shape[0]
    in_count = padded.shape[1]
    w_three = weight.astype(jnp.float32).reshape(out_count, 9, in_count)
    summed = jnp.zeros((padded.shape[0], out_count, row_count, col_count), jnp.float32)
    for step_x in range(3):
        for step_y in range(3):
            window = padded[:, :, step_x:step_x + row_count, step_y:step_y + col_count].astype(jnp.float32)
            summed = summed + jnp.einsum('oc,ncxy->noxy', w_three[:, step_x * 3 + step_y], window)
    return summed

def weight_grad(cotan, padded):
    row_count = cotan.shape[2]
    col_count = cotan.shape[3]
    offset_parts = []
    for step_x in range(3):
        for step_y in range(3):
            window = padded[:, :, step_x:step_x + row_count, step_y:step_y + col_count].astype(jnp.float32)
            offset_parts.append(jnp.einsum('noxy,ncxy->oc', cotan.astype(jnp.float32), window))
    stacked = jnp.stack(offset_parts, axis=1)
    return stacked.reshape(stacked.shape[0], -1)

def spin_contract(cotan, padded):
    row_count = cotan.shape[2]
    col_count = cotan.shape[3]
    offset_parts = []
    for step_x in range(3):
        for step_y in range(3):
            window = padded[:, 0, step_x:step_x + row_count, step_y:step_y + col_count].astype(jnp.float32)
            offset_parts.append(jnp.einsum('ncxy,nxy->c', cotan, window, precision=lax.Precision.HIGHEST))
    return jnp.stack(offset_parts, axis=1)

def flipped(weight):
    out_count = weight.shape[0]
    in_count = weight.shape[1] // 9
    return jnp.transpose(weight.reshape(out_count, 9, in_count)[:, ::-1, :], (2, 1, 0)).reshape(in_count, 9 * out_count)

def silu_slope(pre_act):
    sigmoid_value = jax.nn.sigmoid(pre_act)
    return sigmoid_value * (1.0 + pre_act * (1.0 - sigmoid_value))

def pad_torus(source):
    return jnp.pad(source, ((0, 0), (0, 0), (1, 1), (1, 1)), mode='wrap')

def reference(spins, embed_w, block_w, readout, amp_cot):
    site_scale = 1.0 / math.sqrt(LX * LY)
    spin_pad = pad_torus(spins.astype(jnp.bfloat16)[:, None])
    h_zero = conv_field(spin_pad, embed_w).astype(jnp.bfloat16)

    def one_state(running, scan_inputs):
        w_state, v_state, c_state = scan_inputs
        stream = h_zero.astype(jnp.float32)
        saved_list = []
        for block_index in range(BLOCKS):
            in_pad = pad_torus(stream.astype(jnp.bfloat16))
            z_one = conv_field(in_pad, w_state[block_index, 0])
            g_pad = pad_torus(jax.nn.silu(z_one).astype(jnp.bfloat16))
            stream = stream + conv_field(g_pad, w_state[block_index, 1])
            saved_list.append((in_pad, z_one, g_pad))
        v_float = v_state.astype(jnp.float32)
        part_row = jnp.einsum('c,kcxy->k', v_float, jax.nn.silu(stream), precision=lax.Precision.HIGHEST) * site_scale
        d_stream = (c_state * site_scale)[:, None, None, None] * v_float[None, :, None, None] * silu_slope(stream)
        grad_list = [None] * BLOCKS
        for block_index in reversed(range(BLOCKS)):
            in_pad, z_one, g_pad = saved_list[block_index]
            dz_two = d_stream.astype(jnp.bfloat16)
            grad_two = weight_grad(dz_two, g_pad)
            dg_one = conv_field(pad_torus(dz_two), flipped(w_state[block_index, 1]))
            dz_one = (dg_one * silu_slope(z_one)).astype(jnp.bfloat16)
            grad_one = weight_grad(dz_one, in_pad)
            d_stream = d_stream + conv_field(pad_torus(dz_one), flipped(w_state[block_index, 0]))
            grad_list[block_index] = jnp.stack([grad_one, grad_two])
        return (running + d_stream, (part_row, jnp.stack(grad_list)))
    zero_start = jnp.zeros((WALKERS, C, LX, LY), jnp.float32)
    cot_total, (amp_rows, grad_stack) = lax.scan(one_state, zero_start, (block_w, readout, amp_cot))
    block_grad = jnp.transpose(grad_stack, (0, 3, 1, 2, 4)).reshape(STATES * C, BLOCKS, 2, 9 * C)
    return (amp_rows, block_grad, spin_contract(cot_total, spin_pad))
```

```python
import functools
import math

import jax
import jax.numpy as jnp
from jax import lax
from jax.experimental import pallas as pl
from jax.experimental.pallas import tpu as pltpu
from jax.sharding import Mesh
from jax.sharding import PartitionSpec as P

C = 64
LX = 8
LY = 128
ROWS = 2 * LX
SITES = ROWS * LY
CHUNK = 24
HEAD = 6
SCALE = 1.0 / math.sqrt(LX * LY)
F32 = jnp.float32
BF16 = jnp.bfloat16


def lanes(row):
    return pl.ds(row * LY, LY)


def neighbour(row, step):
    return (row // LX) * LX + (row % LX + step) % LX


def tap_row(tap):
    return tap if tap < 5 else tap + 3


def store_shifted(ref, row, value):
    ref[0:C, lanes(row)] = pltpu.roll(value, 1, 1).astype(BF16)
    ref[C : 2 * C, lanes(row)] = value.astype(BF16)
    ref[2 * C : 3 * C, lanes(row)] = pltpu.roll(value, LY - 1, 1).astype(BF16)


def store_spread(ref, row, value):
    for step in range(3):
        ref[step * C : (step + 1) * C, lanes(neighbour(row, step - 1))] = value


def gather_rows(ref, row):
    return (
        ref[0:C, lanes(neighbour(row, -1))]
        + ref[C : 2 * C, lanes(row)]
        + ref[2 * C : 3 * C, lanes(neighbour(row, 1))]
    )


def gather_cols(ref, row):
    return (
        pltpu.roll(ref[0:C, lanes(row)], LY - 1, 1)
        + ref[C : 2 * C, lanes(row)]
        + pltpu.roll(ref[2 * C : 3 * C, lanes(row)], 1, 1)
    )


def matmul(left, right_ref, out_ref):
    for start in range(0, SITES, 256):
        cols = pl.ds(start, 256)
        out_ref[:, cols] = jnp.dot(left, right_ref[:, cols], preferred_element_type=F32)


def dot_nt(left, right):
    return lax.dot_general(left, right, (((1,), (1,)), ((), ())), preferred_element_type=F32)


def main_kernel(
    spin_ref,
    embed_ref,
    weight_hbm,
    readout_ref,
    cot_ref,
    out_ref,
    w_ref,
    wf_ref,
    wt_ref,
    patch_ref,
    h_ref,
    hc_ref,
    gc_ref,
    d2_ref,
    d1_ref,
    slope_ref,
    stream_ref,
    y_ref,
    sem,
):
    state = lax.axis_index("yh") * 8 + lax.axis_index("z")
    lat = lax.axis_index("yl") * 2 + lax.axis_index("core")
    first_walker = lat * 4 + lax.axis_index("x")
    copy = pltpu.make_async_copy(weight_hbm.at[state, 0], w_ref, sem)
    copy.start()

    patch_ref[...] = jnp.zeros_like(patch_ref)
    spin = spin_ref[...].astype(F32)
    rolled = (pltpu.roll(spin, 1, 1), spin, pltpu.roll(spin, LY - 1, 1))
    for row in range(ROWS):
        for tap in range(9):
            source = neighbour(row, tap // 3 - 1)
            patch_ref[tap_row(tap) : tap_row(tap) + 1, lanes(row)] = rolled[tap % 3][
                source : source + 1, :
            ]
    embed = embed_ref[...].astype(F32)
    embed16 = jnp.concatenate(
        [embed[:, 0:5], jnp.zeros((C, 3), F32), embed[:, 5:9], jnp.zeros((C, 4), F32)], axis=1
    ).astype(BF16)
    patches = patch_ref[...].astype(BF16)
    h_ref[...] = jnp.dot(embed16, patches, preferred_element_type=F32).astype(BF16).astype(F32)
    for row in range(ROWS):
        store_shifted(hc_ref, row, h_ref[:, lanes(row)])

    pick = lax.broadcasted_iota(jnp.int32, (16, C), 0) == state
    readout = jnp.where(pick, readout_ref[...].astype(F32), 0.0)
    column = jnp.sum(jnp.transpose(readout), axis=1, keepdims=True)
    cot_row = jnp.sum(jnp.where(pick, cot_ref[...], 0.0), axis=0, keepdims=True)
    walker_lane = lax.broadcasted_iota(jnp.int32, (1, C), 1)
    cots = [
        jnp.sum(jnp.where(walker_lane == first_walker + 32 * k, cot_row, 0.0), axis=1, keepdims=True)
        * SCALE
        for k in range(2)
    ]

    copy.wait()
    for block in range(2):
        for step in range(3):
            wf_ref[block, step * C : (step + 1) * C, :] = w_ref[block][:, 192 * step : 192 * step + 192]
        wt_ref[block] = jnp.transpose(wf_ref[block].astype(F32)).astype(BF16)

    matmul(wf_ref[0], hc_ref, y_ref)
    for row in range(ROWS):
        z = gather_rows(y_ref, row)
        sig = 1.0 / (1.0 + jnp.exp(-z))
        slope_ref[:, lanes(row)] = sig * (1.0 + z * (1.0 - sig))
        store_shifted(gc_ref, row, (z * sig).astype(BF16).astype(F32))

    matmul(wf_ref[1], gc_ref, y_ref)
    amps = []
    for half in range(2):
        weight = cots[half] * column
        total = jnp.zeros((C, LY), F32)
        for row in range(half * LX, half * LX + LX):
            u = h_ref[:, lanes(row)] + gather_rows(y_ref, row)
            sig = 1.0 / (1.0 + jnp.exp(-u))
            total = total + u * sig
            d = weight * (sig * (1.0 + u * (1.0 - sig)))
            stream_ref[:, lanes(row)] = d
            store_spread(d2_ref, row, d.astype(BF16))
        amps.append(jnp.sum(jnp.sum(total * column, axis=0, keepdims=True), axis=1, keepdims=True) * SCALE)

    grad_two = dot_nt(d2_ref[...], gc_ref[...])
    matmul(wt_ref[1], d2_ref, y_ref)
    for row in range(ROWS):
        dz = (gather_cols(y_ref, row) * slope_ref[:, lanes(row)]).astype(BF16)
        store_spread(d1_ref, row, dz)

    grad_one = dot_nt(d1_ref[...], hc_ref[...])
    matmul(wt_ref[0], d1_ref, y_ref)
    embed_sum = jnp.zeros((16, C), F32)
    for row in range(ROWS):
        dh = stream_ref[:, lanes(row)] + gather_cols(y_ref, row)
        high = dh.astype(BF16)
        low = (dh - high.astype(F32)).astype(BF16)
        mine = patch_ref[:, lanes(row)].astype(BF16)
        embed_sum = embed_sum + (dot_nt(mine, high) + dot_nt(mine, low))

    lane = lax.broadcasted_iota(jnp.int32, (8, 2 * C), 1)
    sub = lax.broadcasted_iota(jnp.int32, (8, 2 * C), 0)
    small = jnp.concatenate([embed_sum[0:8], embed_sum[8:16]], axis=1)
    for k in range(2):
        small = jnp.where((sub == 5) & (lane == first_walker + 32 * k), amps[k], small)
    thirds = (
        grad_one[:, 0:LY],
        grad_two[:, 0:LY],
        jnp.concatenate([grad_one[:, LY:192], grad_two[:, LY:192]], axis=1),
    )
    for chunk in range(32):
        out_ref[chunk * CHUNK : chunk * CHUNK + 8, :] = small
    for third in range(3):
        for step in range(3):
            for upper in range(2):
                place = HEAD + (third * 3 + step) * 2 + upper
                for quarter in range(4):
                    base = step * C + quarter * 16 + upper * 8
                    out_ref[pl.ds(quarter * 8 * CHUNK + place, 8, stride=CHUNK), :] = thirds[third][
                        base : base + 8, :
                    ]


def final_kernel(grad_ref, small_ref, amp_ref, out_ref, embed_ref):
    amp_ref[...] = small_ref[:, 5, 0:C]
    total = jnp.sum(small_ref[...], axis=0)
    stacked = jnp.concatenate([total[:, 0:C], total[:, C : 2 * C]], axis=0)
    turned = jnp.transpose(stacked)
    embed_ref[:, 0:5] = turned[:, 0:5]
    embed_ref[:, 5:9] = turned[:, 8:12]
    for upper in range(2):
        for step in range(3):
            both = grad_ref[:, HEAD + (6 + step) * 2 + upper, :]
            for block in range(2):
                main = grad_ref[:, HEAD + (block * 3 + step) * 2 + upper, :]
                rest = both[:, block * C : (block + 1) * C]
                out_ref[upper * 8 : upper * 8 + 8, 0, block, step * 192 : step * 192 + 192] = (
                    jnp.concatenate([main, rest], axis=1)
                )


def vmem(count):
    return [pl.BlockSpec(memory_space=pltpu.VMEM) for _ in range(count)]


def local(spins, embed_w, block_w, readout, amp_cot):
    own = jnp.broadcast_to(spins, (8, 1, LY))
    by_z = lax.all_to_all(own, "z", 0, 0, tiled=True)
    doubled = jnp.concatenate([by_z, by_z], axis=0)
    both = lax.all_to_all(doubled, ("yh", "yl", "core"), 0, 0, tiled=True).reshape(ROWS, LY)
    wide = (192, SITES)
    payload = pl.pallas_call(
        main_kernel,
        out_shape=jax.ShapeDtypeStruct((32 * CHUNK, LY), F32),
        in_specs=vmem(2) + [pl.BlockSpec(memory_space=pl.ANY)] + vmem(2),
        out_specs=pl.BlockSpec(memory_space=pltpu.VMEM),
        scratch_shapes=[
            pltpu.VMEM((2, C, 576), BF16),
            pltpu.VMEM((2, 192, 192), BF16),
            pltpu.VMEM((2, 192, 192), BF16),
            pltpu.VMEM((16, SITES), F32),
            pltpu.VMEM((C, SITES), F32),
            pltpu.VMEM(wide, BF16),
            pltpu.VMEM(wide, BF16),
            pltpu.VMEM(wide, BF16),
            pltpu.VMEM(wide, BF16),
            pltpu.VMEM((C, SITES), F32),
            pltpu.VMEM((C, SITES), F32),
            pltpu.VMEM(wide, F32),
            pltpu.SemaphoreType.DMA,
        ],
        name="states",
    )(both, embed_w, block_w, readout, amp_cot)
    parts = lax.all_to_all(payload.reshape(32, CHUNK, LY), ("x", "yl", "core"), 0, 0, tiled=True)
    own_sum = jnp.sum(parts, axis=0)
    grads = lax.all_to_all(
        jnp.broadcast_to(own_sum, (8, CHUNK, LY)), ("yl", "core"), 0, 0, tiled=True
    )
    small = lax.all_to_all(
        jnp.broadcast_to(own_sum[0:8], (16, 8, LY)), ("yh", "z"), 0, 0, tiled=True
    )
    return pl.pallas_call(
        final_kernel,
        out_shape=(
            jax.ShapeDtypeStruct((16, C), F32),
            jax.ShapeDtypeStruct((16, 1, 2, 576), F32),
            jax.ShapeDtypeStruct((C, 9), F32),
        ),
        in_specs=vmem(2),
        out_specs=tuple(vmem(3)),
        name="outputs",
    )(grads, small)


def solution(mesh):
    fine = Mesh(mesh.devices.reshape(2, 8, 4, 4, 2), ("yh", "z", "x", "yl", "core"))
    return jax.shard_map(
        local,
        mesh=fine,
        in_specs=(P(("yh", "z", "x"), ("yl", "core"), None), P(), P(), P(), P()),
        out_specs=(P(), P(("yh", "z", "x"), None, None, None), P()),
        check_vma=False,
    )
```

```python
import math

import jax
import jax.numpy as jnp
from jax import lax
from jax.experimental import pallas as pl
from jax.experimental.pallas import tpu as pltpu
from jax.sharding import Mesh
from jax.sharding import PartitionSpec as P

C = 64
LX = 8
LY = 128
ROWS = 2 * LX
SITES = ROWS * LY
CHUNK = 24
HEAD = 6
SCALE = 1.0 / math.sqrt(LX * LY)
F32 = jnp.float32
BF16 = jnp.bfloat16


def lanes(row):
    return pl.ds(row * LY, LY)


def neighbour(row, step):
    return (row // LX) * LX + (row % LX + step) % LX


def tap_row(tap):
    return tap if tap < 5 else tap + 3


def store_shifted(ref, row, value):
    ref[0:C, lanes(row)] = pltpu.roll(value, 1, 1).astype(BF16)
    ref[C : 2 * C, lanes(row)] = value.astype(BF16)
    ref[2 * C : 3 * C, lanes(row)] = pltpu.roll(value, LY - 1, 1).astype(BF16)


def store_spread(ref, row, value):
    for step in range(3):
        ref[step * C : (step + 1) * C, lanes(neighbour(row, step - 1))] = value


def gather_rows(ref, row):
    return (
        ref[0:C, lanes(neighbour(row, -1))]
        + ref[C : 2 * C, lanes(row)]
        + ref[2 * C : 3 * C, lanes(neighbour(row, 1))]
    )


def gather_cols(ref, row):
    return (
        pltpu.roll(ref[0:C, lanes(row)], LY - 1, 1)
        + ref[C : 2 * C, lanes(row)]
        + pltpu.roll(ref[2 * C : 3 * C, lanes(row)], 1, 1)
    )


def matmul(left, right_ref, out_ref):
    for start in range(0, SITES, 256):
        cols = pl.ds(start, 256)
        out_ref[:, cols] = jnp.dot(left, right_ref[:, cols], preferred_element_type=F32)


def dot_nt(left, right):
    return lax.dot_general(left, right, (((1,), (1,)), ((), ())), preferred_element_type=F32)


def main_kernel(
    spin_ref,
    embed_ref,
    weight_hbm,
    readout_ref,
    cot_ref,
    out_ref,
    w_ref,
    wf_ref,
    wt_ref,
    patch_ref,
    h_ref,
    hc_ref,
    gc_ref,
    d2_ref,
    d1_ref,
    slope_ref,
    stream_ref,
    y_ref,
    sem,
):
    state = lax.axis_index("yh") * 8 + lax.axis_index("z")
    lat = lax.axis_index("yl") * 2 + lax.axis_index("core")
    first_walker = lat * 4 + lax.axis_index("x")
    copy = pltpu.make_async_copy(weight_hbm.at[state, 0], w_ref, sem)
    copy.start()

    patch_ref[...] = jnp.zeros_like(patch_ref)
    spin = jnp.concatenate(
        [
            spin_ref[pl.ds(pl.multiple_of(lat * LX + 64 * k, LX), LX), :].astype(F32)
            for k in range(2)
        ],
        axis=0,
    )
    rolled = (pltpu.roll(spin, 1, 1), spin, pltpu.roll(spin, LY - 1, 1))
    for row in range(ROWS):
        for tap in range(9):
            source = neighbour(row, tap // 3 - 1)
            patch_ref[tap_row(tap) : tap_row(tap) + 1, lanes(row)] = rolled[tap % 3][
                source : source + 1, :
            ]
    embed = embed_ref[...].astype(F32)
    embed16 = jnp.transpose(
        jnp.concatenate(
            [embed[0:5], jnp.zeros((3, C), F32), embed[5:9], jnp.zeros((4, C), F32)], axis=0
        )
    ).astype(BF16)
    patches = patch_ref[...].astype(BF16)
    h_ref[...] = jnp.dot(embed16, patches, preferred_element_type=F32).astype(BF16).astype(F32)
    for row in range(ROWS):
        store_shifted(hc_ref, row, h_ref[:, lanes(row)])

    pick = lax.broadcasted_iota(jnp.int32, (16, C), 0) == state
    readout = jnp.where(pick, readout_ref[...].astype(F32), 0.0)
    column = jnp.sum(jnp.transpose(readout), axis=1, keepdims=True)
    cot_row = jnp.sum(jnp.where(pick, cot_ref[...], 0.0), axis=0, keepdims=True)
    walker_lane = lax.broadcasted_iota(jnp.int32, (1, C), 1)
    cots = [
        jnp.sum(jnp.where(walker_lane == first_walker + 32 * k, cot_row, 0.0), axis=1, keepdims=True)
        * SCALE
        for k in range(2)
    ]

    copy.wait()
    for block in range(2):
        for step in range(3):
            wf_ref[block, step * C : (step + 1) * C, :] = w_ref[block][:, 192 * step : 192 * step + 192]
        wt_ref[block] = jnp.transpose(wf_ref[block].astype(F32)).astype(BF16)

    matmul(wf_ref[0], hc_ref, y_ref)
    for row in range(ROWS):
        z = gather_rows(y_ref, row)
        sig = 1.0 / (1.0 + jnp.exp(-z))
        slope_ref[:, lanes(row)] = sig * (1.0 + z * (1.0 - sig))
        store_shifted(gc_ref, row, (z * sig).astype(BF16).astype(F32))

    matmul(wf_ref[1], gc_ref, y_ref)
    amps = []
    for half in range(2):
        weight = cots[half] * column
        total = jnp.zeros((C, LY), F32)
        for row in range(half * LX, half * LX + LX):
            u = h_ref[:, lanes(row)] + gather_rows(y_ref, row)
            sig = 1.0 / (1.0 + jnp.exp(-u))
            total = total + u * sig
            d = weight * (sig * (1.0 + u * (1.0 - sig)))
            stream_ref[:, lanes(row)] = d
            store_spread(d2_ref, row, d.astype(BF16))
        amps.append(jnp.sum(jnp.sum(total * column, axis=0, keepdims=True), axis=1, keepdims=True) * SCALE)

    grad_two = dot_nt(d2_ref[...], gc_ref[...])
    matmul(wt_ref[1], d2_ref, y_ref)
    for row in range(ROWS):
        dz = (gather_cols(y_ref, row) * slope_ref[:, lanes(row)]).astype(BF16)
        store_spread(d1_ref, row, dz)

    grad_one = dot_nt(d1_ref[...], hc_ref[...])
    matmul(wt_ref[0], d1_ref, y_ref)
    embed_sum = jnp.zeros((16, C), F32)
    for row in range(ROWS):
        dh = stream_ref[:, lanes(row)] + gather_cols(y_ref, row)
        high = dh.astype(BF16)
        low = (dh - high.astype(F32)).astype(BF16)
        mine = patch_ref[:, lanes(row)].astype(BF16)
        embed_sum = embed_sum + (dot_nt(mine, high) + dot_nt(mine, low))

    lane = lax.broadcasted_iota(jnp.int32, (8, 2 * C), 1)
    sub = lax.broadcasted_iota(jnp.int32, (8, 2 * C), 0)
    small = jnp.concatenate([embed_sum[0:8], embed_sum[8:16]], axis=1)
    for k in range(2):
        small = jnp.where((sub == 5) & (lane == first_walker + 32 * k), amps[k], small)
    thirds = (
        grad_one[:, 0:LY],
        grad_two[:, 0:LY],
        jnp.concatenate([grad_one[:, LY:192], grad_two[:, LY:192]], axis=1),
    )
    for chunk in range(32):
        out_ref[chunk * CHUNK : chunk * CHUNK + 8, :] = small
    for third in range(3):
        for step in range(3):
            for upper in range(2):
                place = HEAD + (third * 3 + step) * 2 + upper
                for quarter in range(4):
                    base = step * C + quarter * 16 + upper * 8
                    out_ref[pl.ds(quarter * 8 * CHUNK + place, 8, stride=CHUNK), :] = thirds[third][
                        base : base + 8, :
                    ]


def final_kernel(all_ref, amp_ref, out_ref, embed_ref):
    upper_y = lax.axis_index("yh")
    depth = lax.axis_index("z")
    total = jnp.zeros((8, 2 * C), F32)
    for source in range(16):
        rows = all_ref[source, 0:8, :]
        total = total + rows
        plane = (source // 8) * 8 + lax.rem(depth - source % 8 + 8, 8)
        amp_ref[pl.ds(plane, 1), :] = rows[5:6, 0:C]
    embed_ref[0:5, :] = total[0:5, 0:C]
    embed_ref[5:9, :] = total[0:4, C : 2 * C]
    base = upper_y * 8
    for upper in range(2):
        for step in range(3):
            both = all_ref[pl.ds(base, 8), HEAD + (6 + step) * 2 + upper, :]
            for block in range(2):
                main = all_ref[pl.ds(base, 8), HEAD + (block * 3 + step) * 2 + upper, :]
                rest = both[:, block * C : (block + 1) * C]
                out_ref[upper * 8 : upper * 8 + 8, 0, block, step * 192 : step * 192 + 192] = (
                    jnp.concatenate([main, rest], axis=1)
                )


def vmem(count):
    return [pl.BlockSpec(memory_space=pltpu.VMEM) for _ in range(count)]


def shift_pairs():
    pairs = []
    for high in range(2):
        for z in range(8):
            for rest in range(32):
                target = (z + rest % 8) % 8
                pairs.append(((high * 8 + z) * 32 + rest, (high * 8 + target) * 32 + rest))
    return pairs


def local(spins, embed_w, block_w, readout, amp_cot):
    own = jnp.broadcast_to(spins, (128, 1, LY))
    fields = lax.all_to_all(own, ("yh", "z", "yl", "core"), 0, 0, tiled=True).reshape(128, LY)
    wide = (192, SITES)
    payload = pl.pallas_call(
        main_kernel,
        out_shape=jax.ShapeDtypeStruct((32 * CHUNK, LY), F32),
        in_specs=vmem(2) + [pl.BlockSpec(memory_space=pl.ANY)] + vmem(2),
        out_specs=pl.BlockSpec(memory_space=pltpu.VMEM),
        scratch_shapes=[
            pltpu.VMEM((2, C, 576), BF16),
            pltpu.VMEM((2, 192, 192), BF16),
            pltpu.VMEM((2, 192, 192), BF16),
            pltpu.VMEM((16, SITES), F32),
            pltpu.VMEM((C, SITES), F32),
            pltpu.VMEM(wide, BF16),
            pltpu.VMEM(wide, BF16),
            pltpu.VMEM(wide, BF16),
            pltpu.VMEM(wide, BF16),
            pltpu.VMEM((C, SITES), F32),
            pltpu.VMEM((C, SITES), F32),
            pltpu.VMEM(wide, F32),
            pltpu.SemaphoreType.DMA,
        ],
        name="states",
    )(fields, embed_w.T, block_w, readout, amp_cot)
    parts = lax.all_to_all(payload.reshape(32, CHUNK, LY), ("x", "yl", "core"), 0, 0, tiled=True)
    own_sum = jnp.sum(parts, axis=0)
    shifted = lax.ppermute(own_sum, ("yh", "z", "x", "yl", "core"), shift_pairs())
    is_small = lax.broadcasted_iota(jnp.int32, (CHUNK, LY), 0) < HEAD
    mixed = jnp.where(is_small, shifted, own_sum)
    gathered = lax.all_to_all(
        jnp.broadcast_to(mixed, (16, CHUNK, LY)), ("yh", "yl", "core"), 0, 0, tiled=True
    )
    log_amp, block_grad, embed_grad = pl.pallas_call(
        final_kernel,
        out_shape=(
            jax.ShapeDtypeStruct((16, C), F32),
            jax.ShapeDtypeStruct((16, 1, 2, 576), F32),
            jax.ShapeDtypeStruct((9, C), F32),
        ),
        in_specs=vmem(1),
        out_specs=tuple(vmem(3)),
        name="outputs",
    )(gathered)
    return log_amp, block_grad, embed_grad.T


def solution(mesh):
    fine = Mesh(mesh.devices.reshape(2, 8, 4, 4, 2), ("yh", "z", "x", "yl", "core"))
    return jax.shard_map(
        local,
        mesh=fine,
        in_specs=(P(("yh", "z", "x"), ("yl", "core"), None), P(), P(), P(), P()),
        out_specs=(P(), P(("yh", "z", "x"), None, None, None), P()),
        check_vma=False,
    )
```

```python
import math

import jax
import jax.numpy as jnp
from jax import lax
from jax.experimental import pallas as pl
from jax.experimental.pallas import tpu as pltpu
from jax.sharding import Mesh
from jax.sharding import PartitionSpec as P

C = 64
LX = 8
LY = 128
ROWS = 2 * LX
SITES = ROWS * LY
CHUNK = 24
HEAD = 6
SCALE = 1.0 / math.sqrt(LX * LY)
F32 = jnp.float32
BF16 = jnp.bfloat16


def lanes(row):
    return pl.ds(row * LY, LY)


def neighbour(row, step):
    return (row // LX) * LX + (row % LX + step) % LX


def tap_row(tap):
    return tap if tap < 5 else tap + 3


def store_shifted(ref, row, value):
    ref[0:C, lanes(row)] = pltpu.roll(value, 1, 1).astype(BF16)
    ref[C : 2 * C, lanes(row)] = value.astype(BF16)
    ref[2 * C : 3 * C, lanes(row)] = pltpu.roll(value, LY - 1, 1).astype(BF16)


def store_spread(ref, row, value):
    for step in range(3):
        ref[step * C : (step + 1) * C, lanes(neighbour(row, step - 1))] = value


def gather_rows(ref, row):
    return (
        ref[0:C, lanes(neighbour(row, -1))]
        + ref[C : 2 * C, lanes(row)]
        + ref[2 * C : 3 * C, lanes(neighbour(row, 1))]
    )


def gather_cols(ref, row):
    return (
        pltpu.roll(ref[0:C, lanes(row)], LY - 1, 1)
        + ref[C : 2 * C, lanes(row)]
        + pltpu.roll(ref[2 * C : 3 * C, lanes(row)], 1, 1)
    )


def matmul(left, right_ref, out_ref):
    for start in range(0, SITES, 256):
        cols = pl.ds(start, 256)
        out_ref[:, cols] = jnp.dot(left, right_ref[:, cols], preferred_element_type=F32)


def dot_nt(left, right):
    return lax.dot_general(left, right, (((1,), (1,)), ((), ())), preferred_element_type=F32)


def main_kernel(
    spin_ref,
    embed_ref,
    weight_hbm,
    readout_ref,
    cot_ref,
    out_ref,
    w_ref,
    wf_ref,
    wt_ref,
    patch_ref,
    h_ref,
    hc_ref,
    gc_ref,
    d2_ref,
    d1_ref,
    slope_ref,
    stream_ref,
    y_ref,
    sem,
):
    along = lax.axis_index("yl")
    state = lax.axis_index("yh") * 8 + jnp.where(lax.axis_index("core") == 0, along, 7 - along)
    first_walker = lax.axis_index("z") * 4 + lax.axis_index("x")
    copy = pltpu.make_async_copy(weight_hbm.at[state, 0], w_ref, sem)
    copy.start()

    patch_ref[...] = jnp.zeros_like(patch_ref)
    spin = spin_ref[...].astype(F32)
    rolled = (pltpu.roll(spin, 1, 1), spin, pltpu.roll(spin, LY - 1, 1))
    for row in range(ROWS):
        for tap in range(9):
            source = neighbour(row, tap // 3 - 1)
            patch_ref[tap_row(tap) : tap_row(tap) + 1, lanes(row)] = rolled[tap % 3][
                source : source + 1, :
            ]
    embed = embed_ref[...].astype(F32)
    embed16 = jnp.transpose(
        jnp.concatenate(
            [embed[0:5], jnp.zeros((3, C), F32), embed[5:9], jnp.zeros((4, C), F32)], axis=0
        )
    ).astype(BF16)
    patches = patch_ref[...].astype(BF16)
    h_ref[...] = jnp.dot(embed16, patches, preferred_element_type=F32).astype(BF16).astype(F32)
    for row in range(ROWS):
        store_shifted(hc_ref, row, h_ref[:, lanes(row)])

    pick = lax.broadcasted_iota(jnp.int32, (16, C), 0) == state
    readout = jnp.where(pick, readout_ref[...].astype(F32), 0.0)
    column = jnp.sum(jnp.transpose(readout), axis=1, keepdims=True)
    cot_row = jnp.sum(jnp.where(pick, cot_ref[...], 0.0), axis=0, keepdims=True)
    walker_lane = lax.broadcasted_iota(jnp.int32, (1, C), 1)
    cots = [
        jnp.sum(jnp.where(walker_lane == first_walker + 32 * k, cot_row, 0.0), axis=1, keepdims=True)
        * SCALE
        for k in range(2)
    ]

    copy.wait()
    for block in range(2):
        for step in range(3):
            wf_ref[block, step * C : (step + 1) * C, :] = w_ref[block][:, 192 * step : 192 * step + 192]
        wt_ref[block] = jnp.transpose(wf_ref[block].astype(F32)).astype(BF16)

    matmul(wf_ref[0], hc_ref, y_ref)
    for row in range(ROWS):
        z = gather_rows(y_ref, row)
        sig = 1.0 / (1.0 + jnp.exp(-z))
        slope_ref[:, lanes(row)] = sig * (1.0 + z * (1.0 - sig))
        store_shifted(gc_ref, row, (z * sig).astype(BF16).astype(F32))

    matmul(wf_ref[1], gc_ref, y_ref)
    amps = []
    for half in range(2):
        weight = cots[half] * column
        total = jnp.zeros((C, LY), F32)
        for row in range(half * LX, half * LX + LX):
            u = h_ref[:, lanes(row)] + gather_rows(y_ref, row)
            sig = 1.0 / (1.0 + jnp.exp(-u))
            total = total + u * sig
            d = weight * (sig * (1.0 + u * (1.0 - sig)))
            stream_ref[:, lanes(row)] = d
            store_spread(d2_ref, row, d.astype(BF16))
        amps.append(jnp.sum(jnp.sum(total * column, axis=0, keepdims=True), axis=1, keepdims=True) * SCALE)

    grad_two = dot_nt(d2_ref[...], gc_ref[...])
    matmul(wt_ref[1], d2_ref, y_ref)
    for row in range(ROWS):
        dz = (gather_cols(y_ref, row) * slope_ref[:, lanes(row)]).astype(BF16)
        store_spread(d1_ref, row, dz)

    grad_one = dot_nt(d1_ref[...], hc_ref[...])
    matmul(wt_ref[0], d1_ref, y_ref)
    embed_sum = jnp.zeros((16, C), F32)
    for row in range(ROWS):
        dh = stream_ref[:, lanes(row)] + gather_cols(y_ref, row)
        high = dh.astype(BF16)
        low = (dh - high.astype(F32)).astype(BF16)
        mine = patch_ref[:, lanes(row)].astype(BF16)
        embed_sum = embed_sum + (dot_nt(mine, high) + dot_nt(mine, low))

    lane = lax.broadcasted_iota(jnp.int32, (8, 2 * C), 1)
    sub = lax.broadcasted_iota(jnp.int32, (8, 2 * C), 0)
    small = jnp.concatenate([embed_sum[0:8], embed_sum[8:16]], axis=1)
    for k in range(2):
        small = jnp.where((sub == 5) & (lane == first_walker + 32 * k), amps[k], small)
    thirds = (
        grad_one[:, 0:LY],
        grad_two[:, 0:LY],
        jnp.concatenate([grad_one[:, LY:192], grad_two[:, LY:192]], axis=1),
    )
    for chunk in range(32):
        out_ref[chunk * CHUNK : chunk * CHUNK + 8, :] = small
    for third in range(3):
        for step in range(3):
            for upper in range(2):
                place = HEAD + (third * 3 + step) * 2 + upper
                for quarter in range(4):
                    base = step * C + quarter * 16 + upper * 8
                    out_ref[pl.ds(quarter * CHUNK + place, 8, stride=4 * CHUNK), :] = thirds[third][
                        base : base + 8, :
                    ]


def final_kernel(all_ref, amp_ref, out_ref, embed_ref):
    total = jnp.zeros((8, 2 * C), F32)
    for source in range(16):
        rows = all_ref[source, 0:8, :]
        total = total + rows
        state = (source // 8) * 8 + folded(source % 8)
        amp_ref[state : state + 1, :] = rows[5:6, 0:C]
    embed_ref[0:5, :] = total[0:5, 0:C]
    embed_ref[5:9, :] = total[0:4, C : 2 * C]
    base = lax.axis_index("yh") * 8
    for upper in range(2):
        for step in range(3):
            both = all_ref[pl.ds(base, 8), HEAD + (6 + step) * 2 + upper, :]
            for block in range(2):
                main = all_ref[pl.ds(base, 8), HEAD + (block * 3 + step) * 2 + upper, :]
                rest = both[:, block * C : (block + 1) * C]
                value = jnp.concatenate([main, rest], axis=1)
                for source in range(8):
                    place = upper * 8 + (folded(source) + 4) % 8
                    out_ref[place : place + 1, 0, block, step * 192 : step * 192 + 192] = value[
                        source : source + 1
                    ]


def vmem(count):
    return [pl.BlockSpec(memory_space=pltpu.VMEM) for _ in range(count)]


def folded(lat):
    along, core = divmod(lat, 2)
    return 7 - along if core else along


def turn_pairs():
    pairs = []
    for high in range(2):
        for z in range(8):
            for x in range(4):
                for lat in range(8):
                    place = next(k for k in range(8) if folded(k) == (z + 4) % 8)
                    source = ((high * 8 + z) * 4 + x) * 8 + lat
                    target = ((high * 8 + folded(lat)) * 4 + x) * 8 + place
                    pairs.append((source, target))
    return pairs


def local(spins, embed_w, block_w, readout, amp_cot):
    own = jnp.broadcast_to(spins, (16, 1, LY))
    fields = lax.all_to_all(own, ("yh", "yl", "core"), 0, 0, tiled=True).reshape(ROWS, LY)
    wide = (192, SITES)
    payload = pl.pallas_call(
        main_kernel,
        out_shape=jax.ShapeDtypeStruct((32 * CHUNK, LY), F32),
        in_specs=vmem(2) + [pl.BlockSpec(memory_space=pl.ANY)] + vmem(2),
        out_specs=pl.BlockSpec(memory_space=pltpu.VMEM),
        scratch_shapes=[
            pltpu.VMEM((2, C, 576), BF16),
            pltpu.VMEM((2, 192, 192), BF16),
            pltpu.VMEM((2, 192, 192), BF16),
            pltpu.VMEM((16, SITES), F32),
            pltpu.VMEM((C, SITES), F32),
            pltpu.VMEM(wide, BF16),
            pltpu.VMEM(wide, BF16),
            pltpu.VMEM(wide, BF16),
            pltpu.VMEM(wide, BF16),
            pltpu.VMEM((C, SITES), F32),
            pltpu.VMEM((C, SITES), F32),
            pltpu.VMEM(wide, F32),
            pltpu.SemaphoreType.DMA,
        ],
        name="states",
    )(fields, embed_w.T, block_w, readout, amp_cot)
    parts = lax.all_to_all(payload.reshape(32, CHUNK, LY), ("z", "x"), 0, 0, tiled=True)
    own_sum = jnp.sum(parts, axis=0)
    turned = lax.ppermute(own_sum, ("yh", "z", "x", "yl", "core"), turn_pairs())
    is_small = lax.broadcasted_iota(jnp.int32, (CHUNK, LY), 0) < HEAD
    mixed = jnp.where(is_small, own_sum, turned)
    gathered = lax.all_to_all(
        jnp.broadcast_to(mixed, (16, CHUNK, LY)), ("yh", "yl", "core"), 0, 0, tiled=True
    )
    log_amp, block_grad, embed_grad = pl.pallas_call(
        final_kernel,
        out_shape=(
            jax.ShapeDtypeStruct((16, C), F32),
            jax.ShapeDtypeStruct((16, 1, 2, 576), F32),
            jax.ShapeDtypeStruct((9, C), F32),
        ),
        in_specs=vmem(1),
        out_specs=tuple(vmem(3)),
        name="outputs",
    )(gathered)
    return log_amp, block_grad, embed_grad.T


def solution(mesh):
    fine = Mesh(mesh.devices.reshape(2, 8, 4, 4, 2), ("yh", "z", "x", "yl", "core"))
    return jax.shard_map(
        local,
        mesh=fine,
        in_specs=(P(("yh", "z", "x"), ("yl", "core"), None), P(), P(), P(), P()),
        out_specs=(P(), P(("yh", "z", "x"), None, None, None), P()),
        check_vma=False,
    )
```

```python
import math

import jax
import jax.numpy as jnp
from jax import lax
from jax.experimental import pallas as pl
from jax.experimental.pallas import tpu as pltpu
from jax.sharding import Mesh
from jax.sharding import PartitionSpec as P

C = 64
LX = 8
LY = 128
ROWS = 2 * LX
SITES = ROWS * LY
CHUNK = 24
HEAD = 6
SCALE = 1.0 / math.sqrt(LX * LY)
F32 = jnp.float32
BF16 = jnp.bfloat16


def lanes(row):
    return pl.ds(row * LY, LY)


def neighbour(row, step):
    return (row // LX) * LX + (row % LX + step) % LX


def store_shifted(ref, row, value):
    ref[0:C, lanes(row)] = pltpu.roll(value, 1, 1)
    ref[C : 2 * C, lanes(row)] = value
    ref[2 * C : 3 * C, lanes(row)] = pltpu.roll(value, LY - 1, 1)


def store_spread(ref, row, value):
    for step in range(3):
        ref[step * C : (step + 1) * C, lanes(neighbour(row, step - 1))] = value


def gather_rows(ref, row):
    return (
        ref[0:C, lanes(neighbour(row, -1))]
        + ref[C : 2 * C, lanes(row)]
        + ref[2 * C : 3 * C, lanes(neighbour(row, 1))]
    )


def gather_cols(ref, row):
    return (
        pltpu.roll(ref[0:C, lanes(row)], LY - 1, 1)
        + ref[C : 2 * C, lanes(row)]
        + pltpu.roll(ref[2 * C : 3 * C, lanes(row)], 1, 1)
    )


def matmul(left, right_ref, out_ref, half):
    for start in range(half * SITES // 2, (half + 1) * SITES // 2, 256):
        cols = pl.ds(start, 256)
        out_ref[:, cols] = jnp.dot(left, right_ref[:, cols], preferred_element_type=F32)


def dot_nt(left, right):
    return lax.dot_general(left, right, (((1,), (1,)), ((), ())), preferred_element_type=F32)


def sigmoid(v):
    return 1.0 / (1.0 + jnp.exp(-v))


def main_kernel(
    spin_ref,
    embed_ref,
    weight_hbm,
    readout_ref,
    cot_ref,
    out_ref,
    w_ref,
    wf_ref,
    wt_ref,
    pad_ref,
    patch_ref,
    h_ref,
    hc_ref,
    gc_ref,
    d2_ref,
    d1_ref,
    slope_ref,
    stream_ref,
    ya_ref,
    yb_ref,
    parts_ref,
    sem,
):
    along = lax.axis_index("yl")
    state = lax.axis_index("yh") * 8 + jnp.where(lax.axis_index("core") == 0, along, 7 - along)
    first_walker = lax.axis_index("z") * 4 + lax.axis_index("x")
    copy = pltpu.make_async_copy(weight_hbm.at[state, 0], w_ref, sem)
    copy.start()
    halves = [range(half * LX, half * LX + LX) for half in range(2)]

    spin = spin_ref[...].astype(F32)
    for half in range(2):
        turned = pltpu.roll(spin[half * LX : half * LX + LX], 1, 0)
        for step, value in enumerate((pltpu.roll(turned, 1, 1), turned, pltpu.roll(turned, LY - 1, 1))):
            pad_ref[step, half * 16 : half * 16 + 8] = value
            pad_ref[step, half * 16 + 8 : half * 16 + 16] = value
    embed = embed_ref[...].astype(F32)
    nothing = jnp.zeros((5, C), F32)
    rows = []
    for step in range(3):
        rows += [embed[3 * k + step : 3 * k + step + 1] for k in range(3)] + [nothing]
    embed24 = jnp.transpose(jnp.concatenate(rows, axis=0)).astype(BF16)
    for half in range(2):
        for row in halves[half]:
            first = half * 16 + row % LX
            patch_ref[:, lanes(row)] = jnp.concatenate(
                [pad_ref[step, first : first + 8] for step in range(3)], axis=0
            ).astype(BF16)
        for row in halves[half]:
            value = jnp.dot(
                embed24, patch_ref[:, lanes(row)], preferred_element_type=F32
            ).astype(BF16)
            h_ref[:, lanes(row)] = value.astype(F32)
            store_shifted(hc_ref, row, value)

    pick = lax.broadcasted_iota(jnp.int32, (16, C), 0) == state
    readout = jnp.where(pick, readout_ref[...].astype(F32), 0.0)
    column = jnp.sum(jnp.transpose(readout), axis=1, keepdims=True)
    cot_row = jnp.sum(jnp.where(pick, cot_ref[...], 0.0), axis=0, keepdims=True)
    walker_lane = lax.broadcasted_iota(jnp.int32, (1, C), 1)
    cots = [
        jnp.sum(jnp.where(walker_lane == first_walker + 32 * k, cot_row, 0.0), axis=1, keepdims=True)
        * SCALE
        for k in range(2)
    ]

    copy.wait()
    for block in range(2):
        for step in range(3):
            wf_ref[block, step * C : (step + 1) * C, :] = w_ref[block][:, 192 * step : 192 * step + 192]
        wt_ref[block] = jnp.transpose(wf_ref[block].astype(F32)).astype(BF16)

    def first_act(half):
        for row in halves[half]:
            z = gather_rows(ya_ref, row)
            sig = sigmoid(z)
            slope_ref[:, lanes(row)] = sig * (1.0 + z * (1.0 - sig))
            store_shifted(gc_ref, row, (z * sig).astype(BF16))

    def second_act(half):
        weight = cots[half] * column
        total = jnp.zeros((C, LY), F32)
        for row in halves[half]:
            u = h_ref[:, lanes(row)] + gather_rows(yb_ref, row)
            sig = sigmoid(u)
            total = total + u * sig
            d = weight * (sig * (1.0 + u * (1.0 - sig)))
            stream_ref[:, lanes(row)] = d
            store_spread(d2_ref, row, d.astype(BF16))
        return (
            jnp.sum(jnp.sum(total * column, axis=0, keepdims=True), axis=1, keepdims=True) * SCALE
        )

    def first_back(half):
        for row in halves[half]:
            dz = (gather_cols(ya_ref, row) * slope_ref[:, lanes(row)]).astype(BF16)
            store_spread(d1_ref, row, dz)

    def last_back(half):
        for row in halves[half]:
            dh = stream_ref[:, lanes(row)] + gather_cols(yb_ref, row)
            high = dh.astype(BF16)
            parts_ref[0:C, lanes(row)] = high
            parts_ref[C : 2 * C, lanes(row)] = (dh - high.astype(F32)).astype(BF16)

    matmul(wf_ref[0], hc_ref, ya_ref, 0)
    matmul(wf_ref[0], hc_ref, ya_ref, 1)
    first_act(0)
    matmul(wf_ref[1], gc_ref, yb_ref, 0)
    first_act(1)
    matmul(wf_ref[1], gc_ref, yb_ref, 1)
    amps = [second_act(0)]
    matmul(wt_ref[1], d2_ref, ya_ref, 0)
    amps.append(second_act(1))
    matmul(wt_ref[1], d2_ref, ya_ref, 1)
    first_back(0)
    grad_two = dot_nt(d2_ref[...], gc_ref[...])
    matmul(wt_ref[0], d1_ref, yb_ref, 0)
    first_back(1)
    matmul(wt_ref[0], d1_ref, yb_ref, 1)
    last_back(0)
    grad_one = dot_nt(d1_ref[...], hc_ref[...])
    last_back(1)
    both = dot_nt(parts_ref[...], patch_ref[...])
    taps = jnp.transpose(both[0:C] + both[C : 2 * C])

    lane = lax.broadcasted_iota(jnp.int32, (8, 2 * C), 1)
    sub = lax.broadcasted_iota(jnp.int32, (8, 2 * C), 0)
    left = jnp.concatenate([taps[0:3], taps[16:19], jnp.zeros((2, C), F32)], axis=0)
    right = jnp.concatenate([taps[8:11], jnp.zeros((5, C), F32)], axis=0)
    small = jnp.concatenate([left, right], axis=1)
    for k in range(2):
        here = ((sub == 3) | (sub == 4)) & (lane == C + first_walker + 32 * k)
        small = jnp.where(here, amps[k], small)
    thirds = (
        grad_one[:, 0:LY],
        grad_two[:, 0:LY],
        jnp.concatenate([grad_one[:, LY:192], grad_two[:, LY:192]], axis=1),
    )
    for chunk in range(32):
        out_ref[chunk * CHUNK : chunk * CHUNK + 8, :] = small
    for third in range(3):
        for step in range(3):
            for upper in range(2):
                place = HEAD + (third * 3 + step) * 2 + upper
                for quarter in range(4):
                    base = step * C + quarter * 16 + upper * 8
                    out_ref[pl.ds(quarter * CHUNK + place, 8, stride=4 * CHUNK), :] = thirds[third][
                        base : base + 8, :
                    ]


def final_kernel(all_ref, amp_ref, out_ref, embed_ref):
    own = lax.axis_index("yh") * 8
    total = jnp.zeros((8, 2 * C), F32)
    for source in range(8):
        rows = all_ref[source, 0:8, :]
        total = total + rows
        amp_ref[pl.ds(own + folded(source), 1), :] = rows[3:4, C : 2 * C]
        amp_ref[pl.ds(8 - own + folded(source), 1), :] = rows[4:5, C : 2 * C]
    for step in range(3):
        embed_ref[3 * step : 3 * step + 1, :] = total[step : step + 1, 0:C]
        embed_ref[3 * step + 1 : 3 * step + 2, :] = total[step : step + 1, C : 2 * C]
        embed_ref[3 * step + 2 : 3 * step + 3, :] = total[3 + step : 4 + step, 0:C]
    for upper in range(2):
        for step in range(3):
            both = all_ref[:, HEAD + (6 + step) * 2 + upper, :]
            for block in range(2):
                main = all_ref[:, HEAD + (block * 3 + step) * 2 + upper, :]
                rest = both[:, block * C : (block + 1) * C]
                value = jnp.concatenate([main, rest], axis=1)
                for source in range(8):
                    place = upper * 8 + (folded(source) + 4) % 8
                    out_ref[place : place + 1, 0, block, step * 192 : step * 192 + 192] = value[
                        source : source + 1
                    ]


def vmem(count):
    return [pl.BlockSpec(memory_space=pltpu.VMEM) for _ in range(count)]


def folded(lat):
    along, core = divmod(lat, 2)
    return 7 - along if core else along


def turn_pairs():
    pairs = []
    for high in range(2):
        for z in range(8):
            for x in range(4):
                for lat in range(8):
                    place = next(k for k in range(8) if folded(k) == (z + 4) % 8)
                    source = ((high * 8 + z) * 4 + x) * 8 + lat
                    target = ((high * 8 + folded(lat)) * 4 + x) * 8 + place
                    pairs.append((source, target))
    return pairs


def local(spins, embed_w, block_w, readout, amp_cot):
    own = jnp.broadcast_to(spins, (16, 1, LY))
    fields = lax.all_to_all(own, ("yh", "yl", "core"), 0, 0, tiled=True).reshape(ROWS, LY)
    wide = (192, SITES)
    payload = pl.pallas_call(
        main_kernel,
        out_shape=jax.ShapeDtypeStruct((32 * CHUNK, LY), F32),
        in_specs=vmem(2) + [pl.BlockSpec(memory_space=pl.ANY)] + vmem(2),
        out_specs=pl.BlockSpec(memory_space=pltpu.VMEM),
        scratch_shapes=[
            pltpu.VMEM((2, C, 576), BF16),
            pltpu.VMEM((2, 192, 192), BF16),
            pltpu.VMEM((2, 192, 192), BF16),
            pltpu.VMEM((3, 32, LY), F32),
            pltpu.VMEM((24, SITES), BF16),
            pltpu.VMEM((C, SITES), F32),
            pltpu.VMEM(wide, BF16),
            pltpu.VMEM(wide, BF16),
            pltpu.VMEM(wide, BF16),
            pltpu.VMEM(wide, BF16),
            pltpu.VMEM((C, SITES), F32),
            pltpu.VMEM((C, SITES), F32),
            pltpu.VMEM(wide, F32),
            pltpu.VMEM(wide, F32),
            pltpu.VMEM((2 * C, SITES), BF16),
            pltpu.SemaphoreType.DMA,
        ],
        name="states",
    )(fields, embed_w.T, block_w, readout, amp_cot)
    parts = lax.all_to_all(payload.reshape(32, CHUNK, LY), ("z", "x"), 0, 0, tiled=True)
    own_sum = jnp.sum(parts, axis=0)
    turned = lax.ppermute(own_sum, ("yh", "z", "x", "yl", "core"), turn_pairs())
    other = lax.ppermute(own_sum, "yh", [(0, 1), (1, 0)])
    row = lax.broadcasted_iota(jnp.int32, (CHUNK, LY), 0)
    is_right = lax.broadcasted_iota(jnp.int32, (CHUNK, LY), 1) >= C
    small = jnp.where(is_right & (row == 3), own_sum, jnp.where(is_right & (row == 4), other, own_sum + other))
    mixed = jnp.where(row < HEAD, small, turned)
    gathered = lax.all_to_all(
        jnp.broadcast_to(mixed, (8, CHUNK, LY)), ("yl", "core"), 0, 0, tiled=True
    )
    log_amp, block_grad, embed_grad = pl.pallas_call(
        final_kernel,
        out_shape=(
            jax.ShapeDtypeStruct((16, C), F32),
            jax.ShapeDtypeStruct((16, 1, 2, 576), F32),
            jax.ShapeDtypeStruct((9, C), F32),
        ),
        in_specs=vmem(1),
        out_specs=tuple(vmem(3)),
        name="outputs",
    )(gathered)
    return log_amp, block_grad, embed_grad.T


def solution(mesh):
    fine = Mesh(mesh.devices.reshape(2, 8, 4, 4, 2), ("yh", "z", "x", "yl", "core"))
    return jax.shard_map(
        local,
        mesh=fine,
        in_specs=(P(("yh", "z", "x"), ("yl", "core"), None), P(), P(), P(), P()),
        out_specs=(P(), P(("yh", "z", "x"), None, None, None), P()),
        check_vma=False,
    )
```

```python
import math

import jax
import jax.numpy as jnp
from jax import lax
from jax.experimental import pallas as pl
from jax.experimental.pallas import tpu as pltpu
from jax.sharding import Mesh
from jax.sharding import PartitionSpec as P

C = 64
LX = 8
LY = 128
ROWS = 2 * LX
SITES = ROWS * LY
CHUNK = 24
HEAD = 6
SCALE = 1.0 / math.sqrt(LX * LY)
F32 = jnp.float32
BF16 = jnp.bfloat16


def lanes(row):
    return pl.ds(row * LY, LY)


def neighbour(row, step):
    return (row // LX) * LX + (row % LX + step) % LX


def store_shifted(ref, row, value):
    ref[0:C, lanes(row)] = pltpu.roll(value, 1, 1)
    ref[C : 2 * C, lanes(row)] = value
    ref[2 * C : 3 * C, lanes(row)] = pltpu.roll(value, LY - 1, 1)


def store_spread(ref, row, value):
    for step in range(3):
        ref[step * C : (step + 1) * C, lanes(neighbour(row, step - 1))] = value


def gather_rows(ref, row):
    return (
        ref[0:C, lanes(neighbour(row, -1))]
        + ref[C : 2 * C, lanes(row)]
        + ref[2 * C : 3 * C, lanes(neighbour(row, 1))]
    )


def gather_cols(ref, row):
    return (
        pltpu.roll(ref[0:C, lanes(row)], LY - 1, 1)
        + ref[C : 2 * C, lanes(row)]
        + pltpu.roll(ref[2 * C : 3 * C, lanes(row)], 1, 1)
    )


def matmul(left, right_ref, out_ref, half):
    for start in range(half * SITES // 2, (half + 1) * SITES // 2, 256):
        cols = pl.ds(start, 256)
        out_ref[:, cols] = jnp.dot(left, right_ref[:, cols], preferred_element_type=F32)


def dot_nt(left, right):
    return lax.dot_general(left, right, (((1,), (1,)), ((), ())), preferred_element_type=F32)


def sigmoid(v):
    return 1.0 / (1.0 + jnp.exp(-v))


def main_kernel(
    spin_ref,
    embed_ref,
    weight_hbm,
    readout_ref,
    cot_ref,
    out_ref,
    w_ref,
    wf_ref,
    wt_ref,
    pad_ref,
    patch_ref,
    h_ref,
    hc_ref,
    gc_ref,
    d2_ref,
    d1_ref,
    slope_ref,
    stream_ref,
    ya_ref,
    yb_ref,
    parts_ref,
    sem,
):
    along = lax.axis_index("yl")
    state = lax.axis_index("yh") * 8 + jnp.where(lax.axis_index("core") == 0, along, 7 - along)
    first_walker = lax.axis_index("z") * 4 + lax.axis_index("x")
    copy = pltpu.make_async_copy(weight_hbm.at[state, 0], w_ref, sem)
    copy.start()
    halves = [range(half * LX, half * LX + LX) for half in range(2)]

    spin = spin_ref[...].astype(F32)
    for half in range(2):
        turned = pltpu.roll(spin[half * LX : half * LX + LX], 1, 0)
        for step, value in enumerate((pltpu.roll(turned, 1, 1), turned, pltpu.roll(turned, LY - 1, 1))):
            pad_ref[step, half * 16 : half * 16 + 8] = value
            pad_ref[step, half * 16 + 8 : half * 16 + 16] = value
    embed = embed_ref[...].astype(F32)
    nothing = jnp.zeros((5, C), F32)
    rows = []
    for step in range(3):
        rows += [embed[3 * k + step : 3 * k + step + 1] for k in range(3)] + [nothing]
    embed24 = jnp.transpose(jnp.concatenate(rows, axis=0)).astype(BF16)
    for half in range(2):
        for row in halves[half]:
            first = half * 16 + row % LX
            patch_ref[:, lanes(row)] = jnp.concatenate(
                [pad_ref[step, first : first + 8] for step in range(3)], axis=0
            ).astype(BF16)
        for row in halves[half]:
            value = jnp.dot(
                embed24, patch_ref[:, lanes(row)], preferred_element_type=F32
            ).astype(BF16)
            h_ref[:, lanes(row)] = value.astype(F32)
            store_shifted(hc_ref, row, value)

    pick = lax.broadcasted_iota(jnp.int32, (16, C), 0) == state
    readout = jnp.where(pick, readout_ref[...].astype(F32), 0.0)
    column = jnp.sum(jnp.transpose(readout), axis=1, keepdims=True)
    cot_row = jnp.sum(jnp.where(pick, cot_ref[...], 0.0), axis=0, keepdims=True)
    walker_lane = lax.broadcasted_iota(jnp.int32, (1, C), 1)
    cots = [
        jnp.sum(jnp.where(walker_lane == first_walker + 32 * k, cot_row, 0.0), axis=1, keepdims=True)
        * SCALE
        for k in range(2)
    ]

    copy.wait()
    for block in range(2):
        for step in range(3):
            wf_ref[block, step * C : (step + 1) * C, :] = w_ref[block][:, 192 * step : 192 * step + 192]
        wt_ref[block] = jnp.transpose(wf_ref[block].astype(F32)).astype(BF16)

    def first_act(half):
        for row in halves[half]:
            z = gather_rows(ya_ref, row)
            sig = sigmoid(z)
            slope_ref[:, lanes(row)] = sig * (1.0 + z * (1.0 - sig))
            store_shifted(gc_ref, row, (z * sig).astype(BF16))

    def second_act(half):
        weight = cots[half] * column
        total = jnp.zeros((C, LY), F32)
        for row in halves[half]:
            u = h_ref[:, lanes(row)] + gather_rows(yb_ref, row)
            sig = sigmoid(u)
            total = total + u * sig
            d = weight * (sig * (1.0 + u * (1.0 - sig)))
            stream_ref[:, lanes(row)] = d
            store_spread(d2_ref, row, d.astype(BF16))
        return (
            jnp.sum(jnp.sum(total * column, axis=0, keepdims=True), axis=1, keepdims=True) * SCALE
        )

    def first_back(half):
        for row in halves[half]:
            dz = (gather_cols(ya_ref, row) * slope_ref[:, lanes(row)]).astype(BF16)
            store_spread(d1_ref, row, dz)

    def last_back(half):
        for row in halves[half]:
            dh = stream_ref[:, lanes(row)] + gather_cols(yb_ref, row)
            high = dh.astype(BF16)
            parts_ref[0:C, lanes(row)] = high
            parts_ref[C : 2 * C, lanes(row)] = (dh - high.astype(F32)).astype(BF16)

    matmul(wf_ref[0], hc_ref, ya_ref, 0)
    matmul(wf_ref[0], hc_ref, ya_ref, 1)
    first_act(0)
    matmul(wf_ref[1], gc_ref, yb_ref, 0)
    first_act(1)
    matmul(wf_ref[1], gc_ref, yb_ref, 1)
    amps = [second_act(0)]
    matmul(wt_ref[1], d2_ref, ya_ref, 0)
    amps.append(second_act(1))
    matmul(wt_ref[1], d2_ref, ya_ref, 1)
    first_back(0)
    grad_two = dot_nt(d2_ref[...], gc_ref[...])
    matmul(wt_ref[0], d1_ref, yb_ref, 0)
    first_back(1)
    matmul(wt_ref[0], d1_ref, yb_ref, 1)
    last_back(0)
    grad_one = dot_nt(d1_ref[...], hc_ref[...])
    last_back(1)
    both = dot_nt(parts_ref[...], patch_ref[...])
    taps = jnp.transpose(both[0:C] + both[C : 2 * C])

    lane = lax.broadcasted_iota(jnp.int32, (8, 2 * C), 1)
    sub = lax.broadcasted_iota(jnp.int32, (8, 2 * C), 0)
    left = jnp.concatenate([taps[0:3], taps[16:19], jnp.zeros((2, C), F32)], axis=0)
    right = jnp.concatenate([taps[8:11], jnp.zeros((5, C), F32)], axis=0)
    small = jnp.concatenate([left, right], axis=1)
    for k in range(2):
        here = ((sub == 3) | (sub == 4)) & (lane == C + first_walker + 32 * k)
        small = jnp.where(here, amps[k], small)
    thirds = (
        grad_one[:, 0:LY],
        grad_two[:, 0:LY],
        jnp.concatenate([grad_one[:, LY:192], grad_two[:, LY:192]], axis=1),
    )
    for chunk in range(32):
        out_ref[chunk * CHUNK : chunk * CHUNK + 8, :] = small
    for third in range(3):
        for step in range(3):
            for upper in range(2):
                place = HEAD + (third * 3 + step) * 2 + upper
                for quarter in range(4):
                    base = step * C + quarter * 16 + upper * 8
                    out_ref[pl.ds(quarter * CHUNK + place, 8, stride=4 * CHUNK), :] = thirds[third][
                        base : base + 8, :
                    ]


def final_kernel(all_ref, amp_ref, out_ref, embed_ref):
    own = lax.axis_index("yh") * 8
    total = jnp.zeros((8, 2 * C), F32)
    for source in range(8):
        rows = all_ref[source, 0:8, :]
        total = total + rows
        amp_ref[pl.ds(own + folded(source), 1), :] = rows[3:4, C : 2 * C]
        amp_ref[pl.ds(8 - own + folded(7 - source ^ 1), 1), :] = rows[4:5, C : 2 * C]
    for step in range(3):
        embed_ref[3 * step : 3 * step + 1, :] = total[step : step + 1, 0:C]
        embed_ref[3 * step + 1 : 3 * step + 2, :] = total[step : step + 1, C : 2 * C]
        embed_ref[3 * step + 2 : 3 * step + 3, :] = total[3 + step : 4 + step, 0:C]
    for upper in range(2):
        for step in range(3):
            both = all_ref[:, HEAD + (6 + step) * 2 + upper, :]
            for block in range(2):
                main = all_ref[:, HEAD + (block * 3 + step) * 2 + upper, :]
                rest = both[:, block * C : (block + 1) * C]
                value = jnp.concatenate([main, rest], axis=1)
                for source in range(8):
                    place = upper * 8 + (folded(source) + 4) % 8
                    out_ref[place : place + 1, 0, block, step * 192 : step * 192 + 192] = value[
                        source : source + 1
                    ]


def vmem(count):
    return [pl.BlockSpec(memory_space=pltpu.VMEM) for _ in range(count)]


def folded(lat):
    along, core = divmod(lat, 2)
    return 7 - along if core else along


def turn_pairs():
    pairs = []
    for high in range(2):
        for z in range(8):
            for x in range(4):
                for lat in range(8):
                    place = next(k for k in range(8) if folded(k) == (z + 4) % 8)
                    source = ((high * 8 + z) * 4 + x) * 8 + lat
                    target = ((high * 8 + folded(lat)) * 4 + x) * 8 + place
                    pairs.append((source, target))
    return pairs


def local(spins, embed_w, block_w, readout, amp_cot):
    own = jnp.broadcast_to(spins, (16, 1, LY))
    fields = lax.all_to_all(own, ("yh", "yl", "core"), 0, 0, tiled=True).reshape(ROWS, LY)
    fields = pltpu.with_memory_space_constraint(fields, pltpu.VMEM)
    wide = (192, SITES)
    payload = pl.pallas_call(
        main_kernel,
        out_shape=pltpu.VMEM((32 * CHUNK, LY), F32),
        in_specs=vmem(2) + [pl.BlockSpec(memory_space=pl.ANY)] + vmem(2),
        out_specs=pl.BlockSpec(memory_space=pltpu.VMEM),
        scratch_shapes=[
            pltpu.VMEM((2, C, 576), BF16),
            pltpu.VMEM((2, 192, 192), BF16),
            pltpu.VMEM((2, 192, 192), BF16),
            pltpu.VMEM((3, 32, LY), F32),
            pltpu.VMEM((24, SITES), BF16),
            pltpu.VMEM((C, SITES), F32),
            pltpu.VMEM(wide, BF16),
            pltpu.VMEM(wide, BF16),
            pltpu.VMEM(wide, BF16),
            pltpu.VMEM(wide, BF16),
            pltpu.VMEM((C, SITES), F32),
            pltpu.VMEM((C, SITES), F32),
            pltpu.VMEM(wide, F32),
            pltpu.VMEM(wide, F32),
            pltpu.VMEM((2 * C, SITES), BF16),
            pltpu.SemaphoreType.DMA,
        ],
        name="states",
    )(fields, embed_w.T, block_w, readout, amp_cot)
    parts = lax.all_to_all(payload.reshape(32, CHUNK, LY), ("z", "x"), 0, 0, tiled=True)
    own_sum = jnp.sum(parts, axis=0)
    turned = lax.ppermute(own_sum, ("yh", "z", "x", "yl", "core"), turn_pairs())
    other = lax.ppermute(own_sum, ("yh", "yl"), [(y, 7 - y) for y in range(8)])
    row = lax.broadcasted_iota(jnp.int32, (CHUNK, LY), 0)
    is_right = lax.broadcasted_iota(jnp.int32, (CHUNK, LY), 1) >= C
    small = jnp.where(is_right & (row == 3), own_sum, jnp.where(is_right & (row == 4), other, own_sum + other))
    mixed = jnp.where(row < HEAD, small, turned)
    gathered = lax.all_to_all(
        jnp.broadcast_to(mixed, (8, CHUNK, LY)), ("yl", "core"), 0, 0, tiled=True
    )
    gathered = pltpu.with_memory_space_constraint(gathered, pltpu.VMEM)
    log_amp, block_grad, embed_grad = pl.pallas_call(
        final_kernel,
        out_shape=(
            jax.ShapeDtypeStruct((16, C), F32),
            jax.ShapeDtypeStruct((16, 1, 2, 576), F32),
            jax.ShapeDtypeStruct((9, C), F32),
        ),
        in_specs=vmem(1),
        out_specs=tuple(vmem(3)),
        name="outputs",
    )(gathered)
    return log_amp, block_grad, embed_grad.T


def solution(mesh):
    fine = Mesh(mesh.devices.reshape(2, 8, 4, 4, 2), ("yh", "z", "x", "yl", "core"))
    return jax.shard_map(
        local,
        mesh=fine,
        in_specs=(P(("yh", "z", "x"), ("yl", "core"), None), P(), P(), P(), P()),
        out_specs=(P(), P(("yh", "z", "x"), None, None, None), P()),
        check_vma=False,
    )
```

```python
import math

import jax
import jax.numpy as jnp
from jax import lax
from jax.experimental import pallas as pl
from jax.experimental.pallas import tpu as pltpu
from jax.sharding import Mesh
from jax.sharding import PartitionSpec as P

C = 64
LX = 8
LY = 128
ROWS = 2 * LX
SITES = ROWS * LY
CHUNK = 24
HEAD = 6
SCALE = 1.0 / math.sqrt(LX * LY)
F32 = jnp.float32
BF16 = jnp.bfloat16


def lanes(row):
    return pl.ds(row * LY, LY)


def neighbour(row, step):
    return (row // LX) * LX + (row % LX + step) % LX


def store_shifted(ref, row, value):
    ref[0:C, lanes(row)] = pltpu.roll(value, 1, 1)
    ref[C : 2 * C, lanes(row)] = value
    ref[2 * C : 3 * C, lanes(row)] = pltpu.roll(value, LY - 1, 1)


def store_spread(ref, row, value):
    for step in range(3):
        ref[step * C : (step + 1) * C, lanes(neighbour(row, step - 1))] = value


def gather_rows(ref, row):
    return (
        ref[0:C, lanes(neighbour(row, -1))]
        + ref[C : 2 * C, lanes(row)]
        + ref[2 * C : 3 * C, lanes(neighbour(row, 1))]
    )


def gather_cols(ref, row):
    return (
        pltpu.roll(ref[0:C, lanes(row)], LY - 1, 1)
        + ref[C : 2 * C, lanes(row)]
        + pltpu.roll(ref[2 * C : 3 * C, lanes(row)], 1, 1)
    )


def matmul(left, right_ref, out_ref, half):
    for start in range(half * SITES // 2, (half + 1) * SITES // 2, 256):
        cols = pl.ds(start, 256)
        out_ref[:, cols] = jnp.dot(left, right_ref[:, cols], preferred_element_type=F32)


def dot_nt(left, right):
    return lax.dot_general(left, right, (((1,), (1,)), ((), ())), preferred_element_type=F32)


def sigmoid(v):
    return 1.0 / (1.0 + jnp.exp(-v))


def own_state():
    along = lax.axis_index("yl")
    return lax.axis_index("yh") * 8 + jnp.where(lax.axis_index("core") == 0, along, 7 - along)


def own_walker():
    return lax.axis_index("z") * 4 + lax.axis_index("x")


def weights_kernel(
    embed_ref, weight_hbm, readout_ref, cot_ref, wf_ref, wt_ref, taps_ref, column_ref, w_ref, sem
):
    state = own_state()
    copy = pltpu.make_async_copy(weight_hbm.at[state, 0], w_ref, sem)
    copy.start()
    embed = embed_ref[...].astype(F32)
    nothing = jnp.zeros((5, C), F32)
    rows = []
    for step in range(3):
        rows += [embed[3 * k + step : 3 * k + step + 1] for k in range(3)] + [nothing]
    taps_ref[...] = jnp.transpose(jnp.concatenate(rows, axis=0)).astype(BF16)

    pick = lax.broadcasted_iota(jnp.int32, (16, C), 0) == state
    readout = jnp.where(pick, readout_ref[...].astype(F32), 0.0)
    column = jnp.sum(jnp.transpose(readout), axis=1, keepdims=True)
    cot_row = jnp.sum(jnp.where(pick, cot_ref[...], 0.0), axis=0, keepdims=True)
    walker_lane = lax.broadcasted_iota(jnp.int32, (1, C), 1)
    columns = [column]
    for k in range(2):
        mine = jnp.where(walker_lane == own_walker() + 32 * k, cot_row, 0.0)
        columns.append(jnp.sum(mine, axis=1, keepdims=True) * SCALE * column)
    for k in range(3):
        column_ref[k] = jnp.broadcast_to(columns[k], (C, LY))

    copy.wait()
    for block in range(2):
        for step in range(3):
            wf_ref[block, step * C : (step + 1) * C, :] = w_ref[block][:, 192 * step : 192 * step + 192]
        wt_ref[block] = jnp.transpose(wf_ref[block].astype(F32)).astype(BF16)


def states_kernel(
    spin_ref,
    wf_ref,
    wt_ref,
    taps_ref,
    column_ref,
    out_ref,
    pad_ref,
    patch_ref,
    h_ref,
    hc_ref,
    gc_ref,
    d2_ref,
    d1_ref,
    slope_ref,
    stream_ref,
    ya_ref,
    yb_ref,
    parts_ref,
):
    first_walker = own_walker()
    halves = [range(half * LX, half * LX + LX) for half in range(2)]

    spin = spin_ref[...].astype(F32)
    for half in range(2):
        turned = pltpu.roll(spin[half * LX : half * LX + LX], 1, 0)
        for step, value in enumerate((pltpu.roll(turned, 1, 1), turned, pltpu.roll(turned, LY - 1, 1))):
            pad_ref[step, half * 16 : half * 16 + 8] = value
            pad_ref[step, half * 16 + 8 : half * 16 + 16] = value
    embed24 = taps_ref[...]
    for half in range(2):
        for row in halves[half]:
            first = half * 16 + row % LX
            patch_ref[:, lanes(row)] = jnp.concatenate(
                [pad_ref[step, first : first + 8] for step in range(3)], axis=0
            ).astype(BF16)
        for row in halves[half]:
            value = jnp.dot(
                embed24, patch_ref[:, lanes(row)], preferred_element_type=F32
            ).astype(BF16)
            h_ref[:, lanes(row)] = value.astype(F32)
            store_shifted(hc_ref, row, value)

    def first_act(half):
        for row in halves[half]:
            z = gather_rows(ya_ref, row)
            sig = sigmoid(z)
            slope_ref[:, lanes(row)] = sig * (1.0 + z * (1.0 - sig))
            store_shifted(gc_ref, row, (z * sig).astype(BF16))

    def second_act(half):
        weight = column_ref[1 + half]
        total = jnp.zeros((C, LY), F32)
        for row in halves[half]:
            u = h_ref[:, lanes(row)] + gather_rows(yb_ref, row)
            sig = sigmoid(u)
            total = total + u * sig
            d = weight * (sig * (1.0 + u * (1.0 - sig)))
            stream_ref[:, lanes(row)] = d
            store_spread(d2_ref, row, d.astype(BF16))
        return (
            jnp.sum(jnp.sum(total * column_ref[0], axis=0, keepdims=True), axis=1, keepdims=True) * SCALE
        )

    def first_back(half):
        for row in halves[half]:
            dz = (gather_cols(ya_ref, row) * slope_ref[:, lanes(row)]).astype(BF16)
            store_spread(d1_ref, row, dz)

    def last_back(half):
        for row in halves[half]:
            dh = stream_ref[:, lanes(row)] + gather_cols(yb_ref, row)
            high = dh.astype(BF16)
            parts_ref[0:C, lanes(row)] = high
            parts_ref[C : 2 * C, lanes(row)] = (dh - high.astype(F32)).astype(BF16)

    matmul(wf_ref[0], hc_ref, ya_ref, 0)
    matmul(wf_ref[0], hc_ref, ya_ref, 1)
    first_act(0)
    matmul(wf_ref[1], gc_ref, yb_ref, 0)
    first_act(1)
    matmul(wf_ref[1], gc_ref, yb_ref, 1)
    amps = [second_act(0)]
    matmul(wt_ref[1], d2_ref, ya_ref, 0)
    amps.append(second_act(1))
    matmul(wt_ref[1], d2_ref, ya_ref, 1)
    first_back(0)
    grad_two = dot_nt(d2_ref[...], gc_ref[...])
    matmul(wt_ref[0], d1_ref, yb_ref, 0)
    first_back(1)
    matmul(wt_ref[0], d1_ref, yb_ref, 1)
    last_back(0)
    grad_one = dot_nt(d1_ref[...], hc_ref[...])
    last_back(1)
    both = dot_nt(parts_ref[...], patch_ref[...])
    taps = jnp.transpose(both[0:C] + both[C : 2 * C])

    lane = lax.broadcasted_iota(jnp.int32, (8, 2 * C), 1)
    sub = lax.broadcasted_iota(jnp.int32, (8, 2 * C), 0)
    left = jnp.concatenate([taps[0:3], taps[16:19], jnp.zeros((2, C), F32)], axis=0)
    right = jnp.concatenate([taps[8:11], jnp.zeros((5, C), F32)], axis=0)
    small = jnp.concatenate([left, right], axis=1)
    for k in range(2):
        here = ((sub == 3) | (sub == 4)) & (lane == C + first_walker + 32 * k)
        small = jnp.where(here, amps[k], small)
    thirds = (
        grad_one[:, 0:LY],
        grad_two[:, 0:LY],
        jnp.concatenate([grad_one[:, LY:192], grad_two[:, LY:192]], axis=1),
    )
    for chunk in range(32):
        out_ref[chunk * CHUNK : chunk * CHUNK + 8, :] = small
    for third in range(3):
        for step in range(3):
            for upper in range(2):
                place = HEAD + (third * 3 + step) * 2 + upper
                for quarter in range(4):
                    base = step * C + quarter * 16 + upper * 8
                    out_ref[pl.ds(quarter * CHUNK + place, 8, stride=4 * CHUNK), :] = thirds[third][
                        base : base + 8, :
                    ]


def final_kernel(all_ref, amp_ref, out_ref, embed_ref):
    own = lax.axis_index("yh") * 8
    total = jnp.zeros((8, 2 * C), F32)
    for source in range(8):
        rows = all_ref[source, 0:8, :]
        total = total + rows
        amp_ref[pl.ds(own + folded(source), 1), :] = rows[3:4, C : 2 * C]
        amp_ref[pl.ds(8 - own + folded(7 - source ^ 1), 1), :] = rows[4:5, C : 2 * C]
    for step in range(3):
        embed_ref[3 * step : 3 * step + 1, :] = total[step : step + 1, 0:C]
        embed_ref[3 * step + 1 : 3 * step + 2, :] = total[step : step + 1, C : 2 * C]
        embed_ref[3 * step + 2 : 3 * step + 3, :] = total[3 + step : 4 + step, 0:C]
    for upper in range(2):
        for step in range(3):
            both = all_ref[:, HEAD + (6 + step) * 2 + upper, :]
            for block in range(2):
                main = all_ref[:, HEAD + (block * 3 + step) * 2 + upper, :]
                rest = both[:, block * C : (block + 1) * C]
                value = jnp.concatenate([main, rest], axis=1)
                for source in range(8):
                    place = upper * 8 + (folded(source) + 4) % 8
                    out_ref[place : place + 1, 0, block, step * 192 : step * 192 + 192] = value[
                        source : source + 1
                    ]


def vmem(count):
    return [pl.BlockSpec(memory_space=pltpu.VMEM) for _ in range(count)]


def folded(lat):
    along, core = divmod(lat, 2)
    return 7 - along if core else along


def turn_pairs():
    pairs = []
    for high in range(2):
        for z in range(8):
            for x in range(4):
                for lat in range(8):
                    place = next(k for k in range(8) if folded(k) == (z + 4) % 8)
                    source = ((high * 8 + z) * 4 + x) * 8 + lat
                    target = ((high * 8 + folded(lat)) * 4 + x) * 8 + place
                    pairs.append((source, target))
    return pairs


def local(spins, embed_w, block_w, readout, amp_cot):
    own = jnp.broadcast_to(spins, (16, 1, LY))
    fields = lax.all_to_all(own, ("yh", "yl", "core"), 0, 0, tiled=True).reshape(ROWS, LY)
    fields = pltpu.with_memory_space_constraint(fields, pltpu.VMEM)
    wide = (192, SITES)
    weights = pl.pallas_call(
        weights_kernel,
        out_shape=(
            pltpu.VMEM((2, 192, 192), BF16),
            pltpu.VMEM((2, 192, 192), BF16),
            pltpu.VMEM((C, 24), BF16),
            pltpu.VMEM((3, C, LY), F32),
        ),
        in_specs=vmem(1) + [pl.BlockSpec(memory_space=pl.ANY)] + vmem(2),
        out_specs=tuple(vmem(4)),
        scratch_shapes=[pltpu.VMEM((2, C, 576), BF16), pltpu.SemaphoreType.DMA],
        name="weights",
    )(embed_w.T, block_w, readout, amp_cot)
    weights = [pltpu.with_memory_space_constraint(value, pltpu.VMEM) for value in weights]
    payload = pl.pallas_call(
        states_kernel,
        out_shape=pltpu.VMEM((32 * CHUNK, LY), F32),
        in_specs=vmem(5),
        out_specs=pl.BlockSpec(memory_space=pltpu.VMEM),
        scratch_shapes=[
            pltpu.VMEM((3, 32, LY), F32),
            pltpu.VMEM((24, SITES), BF16),
            pltpu.VMEM((C, SITES), F32),
            pltpu.VMEM(wide, BF16),
            pltpu.VMEM(wide, BF16),
            pltpu.VMEM(wide, BF16),
            pltpu.VMEM(wide, BF16),
            pltpu.VMEM((C, SITES), F32),
            pltpu.VMEM((C, SITES), F32),
            pltpu.VMEM(wide, F32),
            pltpu.VMEM(wide, F32),
            pltpu.VMEM((2 * C, SITES), BF16),
        ],
        name="states",
    )(fields, *weights)
    parts = lax.all_to_all(payload.reshape(32, CHUNK, LY), ("z", "x"), 0, 0, tiled=True)
    own_sum = jnp.sum(parts, axis=0)
    turned = lax.ppermute(own_sum, ("yh", "z", "x", "yl", "core"), turn_pairs())
    other = lax.ppermute(own_sum, ("yh", "yl"), [(y, 7 - y) for y in range(8)])
    row = lax.broadcasted_iota(jnp.int32, (CHUNK, LY), 0)
    own_sum, row, column = lax.optimization_barrier((own_sum, row, lax.broadcasted_iota(jnp.int32, (CHUNK, LY), 1)))
    is_right = column >= C
    small = jnp.where(is_right & (row == 3), own_sum, jnp.where(is_right & (row == 4), other, own_sum + other))
    mixed = jnp.where(row < HEAD, small, turned)
    gathered = lax.all_to_all(
        jnp.broadcast_to(mixed, (8, CHUNK, LY)), ("yl", "core"), 0, 0, tiled=True
    )
    gathered = pltpu.with_memory_space_constraint(gathered, pltpu.VMEM)
    log_amp, block_grad, embed_grad = pl.pallas_call(
        final_kernel,
        out_shape=(
            jax.ShapeDtypeStruct((16, C), F32),
            jax.ShapeDtypeStruct((16, 1, 2, 576), F32),
            jax.ShapeDtypeStruct((9, C), F32),
        ),
        in_specs=vmem(1),
        out_specs=tuple(vmem(3)),
        name="outputs",
    )(gathered)
    return log_amp, block_grad, embed_grad.T


def solution(mesh):
    fine = Mesh(mesh.devices.reshape(2, 8, 4, 4, 2), ("yh", "z", "x", "yl", "core"))
    return jax.shard_map(
        local,
        mesh=fine,
        in_specs=(P(("yh", "z", "x"), ("yl", "core"), None), P(), P(), P(), P()),
        out_specs=(P(), P(("yh", "z", "x"), None, None, None), P()),
        check_vma=False,
    )
```

```python
import math

import jax
import jax.numpy as jnp
from jax import lax
from jax.experimental import pallas as pl
from jax.experimental.pallas import tpu as pltpu
from jax.sharding import Mesh
from jax.sharding import PartitionSpec as P

C = 64
LX = 8
LY = 128
ROWS = 2 * LX
SITES = ROWS * LY
CHUNK = 24
HEAD = 6
SCALE = 1.0 / math.sqrt(LX * LY)
F32 = jnp.float32
BF16 = jnp.bfloat16


def lanes(row):
    return pl.ds(row * LY, LY)


def neighbour(row, step):
    return (row // LX) * LX + (row % LX + step) % LX


def store_shifted(ref, row, value):
    ref[0:C, lanes(row)] = pltpu.roll(value, 1, 1)
    ref[C : 2 * C, lanes(row)] = value
    ref[2 * C : 3 * C, lanes(row)] = pltpu.roll(value, LY - 1, 1)


def store_spread(ref, row, value):
    for step in range(3):
        ref[step * C : (step + 1) * C, lanes(neighbour(row, step - 1))] = value


def gather_rows(ref, row):
    return (
        ref[0:C, lanes(neighbour(row, -1))]
        + ref[C : 2 * C, lanes(row)]
        + ref[2 * C : 3 * C, lanes(neighbour(row, 1))]
    )


def gather_cols(ref, row):
    return (
        pltpu.roll(ref[0:C, lanes(row)], LY - 1, 1)
        + ref[C : 2 * C, lanes(row)]
        + pltpu.roll(ref[2 * C : 3 * C, lanes(row)], 1, 1)
    )


def matmul(left, right_ref, out_ref, half):
    for start in range(half * SITES // 2, (half + 1) * SITES // 2, 256):
        cols = pl.ds(start, 256)
        out_ref[:, cols] = jnp.dot(left, right_ref[:, cols], preferred_element_type=F32)


def dot_nt(left, right):
    return lax.dot_general(left, right, (((1,), (1,)), ((), ())), preferred_element_type=F32)


def sigmoid(v):
    return 1.0 / (1.0 + jnp.exp(-v))


def state_of(which):
    along = lax.axis_index("yl")
    high = lax.axis_index("yh")
    high = high if which == 0 else 1 - high
    return high * 8 + jnp.where(lax.axis_index("core") == 0, along, 7 - along)


def own_walker():
    return lax.axis_index("z") * 4 + lax.axis_index("x")


def weights_kernel(
    embed_ref, weight_hbm, readout_ref, cot_ref, wf_ref, wt_ref, taps_ref, column_ref, w_ref, sem
):
    copies = []
    for which in range(2):
        copy = pltpu.make_async_copy(
            weight_hbm.at[state_of(which), 0], w_ref.at[which], sem.at[which]
        )
        copy.start()
        copies.append(copy)
    embed = embed_ref[...].astype(F32)
    nothing = jnp.zeros((5, C), F32)
    rows = []
    for step in range(3):
        rows += [embed[3 * k + step : 3 * k + step + 1] for k in range(3)] + [nothing]
    taps_ref[...] = jnp.transpose(jnp.concatenate(rows, axis=0)).astype(BF16)

    walker_lane = lax.broadcasted_iota(jnp.int32, (1, C), 1)
    for which in range(2):
        pick = lax.broadcasted_iota(jnp.int32, (16, C), 0) == state_of(which)
        readout = jnp.where(pick, readout_ref[...].astype(F32), 0.0)
        column = jnp.sum(jnp.transpose(readout), axis=1, keepdims=True)
        cot_row = jnp.sum(jnp.where(pick, cot_ref[...], 0.0), axis=0, keepdims=True)
        columns = [column]
        for k in range(2):
            mine = jnp.where(walker_lane == own_walker() + 32 * k, cot_row, 0.0)
            columns.append(jnp.sum(mine, axis=1, keepdims=True) * SCALE * column)
        for k in range(3):
            column_ref[which, k] = jnp.broadcast_to(columns[k], (C, LY))

    for which in range(2):
        copies[which].wait()
        for block in range(2):
            for step in range(3):
                wf_ref[which, block, step * C : (step + 1) * C, :] = w_ref[which, block][
                    :, 192 * step : 192 * step + 192
                ]
            wt_ref[which, block] = jnp.transpose(wf_ref[which, block].astype(F32)).astype(BF16)


def states_kernel(
    spin_ref,
    wf_ref,
    wt_ref,
    taps_ref,
    column_ref,
    out_ref,
    pad_ref,
    patch_ref,
    h_ref,
    hc_ref,
    gc_ref,
    d2_ref,
    d1_ref,
    slope_ref,
    stream_ref,
    ya_ref,
    yb_ref,
    parts_ref,
):
    first_walker = own_walker()
    halves = [range(half * LX, half * LX + LX) for half in range(2)]

    spin = spin_ref[...].astype(F32)
    for half in range(2):
        turned = pltpu.roll(spin[half * LX : half * LX + LX], 1, 0)
        for step, value in enumerate((pltpu.roll(turned, 1, 1), turned, pltpu.roll(turned, LY - 1, 1))):
            pad_ref[step, half * 16 : half * 16 + 8] = value
            pad_ref[step, half * 16 + 8 : half * 16 + 16] = value
    embed24 = taps_ref[...]
    for half in range(2):
        for row in halves[half]:
            first = half * 16 + row % LX
            patch_ref[:, lanes(row)] = jnp.concatenate(
                [pad_ref[step, first : first + 8] for step in range(3)], axis=0
            ).astype(BF16)
        for row in halves[half]:
            value = jnp.dot(
                embed24, patch_ref[:, lanes(row)], preferred_element_type=F32
            ).astype(BF16)
            h_ref[:, lanes(row)] = value.astype(F32)
            store_shifted(hc_ref, row, value)

    def first_act(which, half):
        for row in halves[half]:
            z = gather_rows(ya_ref.at[which], row)
            sig = sigmoid(z)
            slope_ref[which, :, lanes(row)] = sig * (1.0 + z * (1.0 - sig))
            store_shifted(gc_ref.at[which], row, (z * sig).astype(BF16))

    def second_act(which, half):
        weight = column_ref[which, 1 + half]
        total = jnp.zeros((C, LY), F32)
        for row in halves[half]:
            u = h_ref[:, lanes(row)] + gather_rows(yb_ref.at[which], row)
            sig = sigmoid(u)
            total = total + u * sig
            d = weight * (sig * (1.0 + u * (1.0 - sig)))
            stream_ref[which, :, lanes(row)] = d
            store_spread(d2_ref.at[which], row, d.astype(BF16))
        total = jnp.sum(total * column_ref[which, 0], axis=0, keepdims=True)
        return jnp.sum(total, axis=1, keepdims=True) * SCALE

    def first_back(which, half):
        for row in halves[half]:
            dz = gather_cols(ya_ref.at[which], row) * slope_ref[which, :, lanes(row)]
            store_spread(d1_ref.at[which], row, dz.astype(BF16))

    def last_back(half):
        for row in halves[half]:
            sums = [
                stream_ref[which, :, lanes(row)] + gather_cols(yb_ref.at[which], row)
                for which in range(2)
            ]
            dh = sums[0] + sums[1]
            high = dh.astype(BF16)
            parts_ref[0:C, lanes(row)] = high
            parts_ref[C : 2 * C, lanes(row)] = (dh - high.astype(F32)).astype(BF16)

    def store_thirds(third, value):
        for step in range(3):
            for upper in range(2):
                place = HEAD + (third * 3 + step) * 2 + upper
                for quarter in range(4):
                    base = step * C + quarter * 16 + upper * 8
                    out_ref[pl.ds(quarter * CHUNK + place, 8, stride=4 * CHUNK), :] = value[
                        base : base + 8, :
                    ]

    pairs = [(which, half) for which in range(2) for half in range(2)]
    for which, half in pairs:
        matmul(wf_ref[which, 0], hc_ref, ya_ref.at[which], half)
    for which, half in pairs:
        first_act(which, half)
        matmul(wf_ref[which, 1], gc_ref.at[which], yb_ref.at[which], half)
    amps = {}
    for which, half in pairs:
        amps[which, half] = second_act(which, half)
        matmul(wt_ref[which, 1], d2_ref.at[which], ya_ref.at[which], half)
    grad_two = dot_nt(d2_ref[0], gc_ref[0])
    for which, half in pairs:
        first_back(which, half)
        matmul(wt_ref[which, 0], d1_ref.at[which], yb_ref.at[which], half)
    grad_one = dot_nt(d1_ref[0], hc_ref[...])
    last_back(0)
    last_back(1)
    both = dot_nt(parts_ref[...], patch_ref[...])
    taps = jnp.transpose(both[0:C] + both[C : 2 * C])

    lane = lax.broadcasted_iota(jnp.int32, (8, 2 * C), 1)
    sub = lax.broadcasted_iota(jnp.int32, (8, 2 * C), 0)
    left = jnp.concatenate([taps[0:3], taps[16:19], jnp.zeros((2, C), F32)], axis=0)
    right = jnp.concatenate([taps[8:11], jnp.zeros((5, C), F32)], axis=0)
    small = jnp.concatenate([left, right], axis=1)
    for which, half in pairs:
        here = (sub == 3 + which) & (lane == C + first_walker + 32 * half)
        small = jnp.where(here, amps[which, half], small)
    for chunk in range(32):
        out_ref[chunk * CHUNK : chunk * CHUNK + 8, :] = small
    store_thirds(0, grad_one[:, 0:LY])
    store_thirds(1, grad_two[:, 0:LY])
    store_thirds(2, jnp.concatenate([grad_one[:, LY:192], grad_two[:, LY:192]], axis=1))


def final_kernel(all_ref, amp_ref, out_ref, embed_ref):
    own = lax.axis_index("yh") * 8
    total = jnp.zeros((8, 2 * C), F32)
    for source in range(8):
        rows = all_ref[source, 0:8, :]
        total = total + rows
        amp_ref[pl.ds(own + folded(source), 1), :] = rows[3:4, C : 2 * C]
        amp_ref[pl.ds(8 - own + folded(source), 1), :] = rows[4:5, C : 2 * C]
    for step in range(3):
        embed_ref[3 * step : 3 * step + 1, :] = total[step : step + 1, 0:C]
        embed_ref[3 * step + 1 : 3 * step + 2, :] = total[step : step + 1, C : 2 * C]
        embed_ref[3 * step + 2 : 3 * step + 3, :] = total[3 + step : 4 + step, 0:C]
    for upper in range(2):
        for step in range(3):
            both = all_ref[:, HEAD + (6 + step) * 2 + upper, :]
            for block in range(2):
                main = all_ref[:, HEAD + (block * 3 + step) * 2 + upper, :]
                rest = both[:, block * C : (block + 1) * C]
                value = jnp.concatenate([main, rest], axis=1)
                for source in range(8):
                    place = upper * 8 + (folded(source) + 4) % 8
                    out_ref[place : place + 1, 0, block, step * 192 : step * 192 + 192] = value[
                        source : source + 1
                    ]


def vmem(count):
    return [pl.BlockSpec(memory_space=pltpu.VMEM) for _ in range(count)]


def folded(lat):
    along, core = divmod(lat, 2)
    return 7 - along if core else along


def turn_pairs():
    pairs = []
    for high in range(2):
        for z in range(8):
            for x in range(4):
                for lat in range(8):
                    place = next(k for k in range(8) if folded(k) == (z + 4) % 8)
                    source = ((high * 8 + z) * 4 + x) * 8 + lat
                    target = ((high * 8 + folded(lat)) * 4 + x) * 8 + place
                    pairs.append((source, target))
    return pairs


def local(spins, embed_w, block_w, readout, amp_cot):
    own = jnp.broadcast_to(spins, (16, 1, LY))
    fields = lax.all_to_all(own, ("yh", "yl", "core"), 0, 0, tiled=True).reshape(ROWS, LY)
    fields = pltpu.with_memory_space_constraint(fields, pltpu.VMEM)
    pair = (2, 192, SITES)
    weights = pl.pallas_call(
        weights_kernel,
        out_shape=(
            pltpu.VMEM((2, 2, 192, 192), BF16),
            pltpu.VMEM((2, 2, 192, 192), BF16),
            pltpu.VMEM((C, 24), BF16),
            pltpu.VMEM((2, 3, C, LY), F32),
        ),
        in_specs=vmem(1) + [pl.BlockSpec(memory_space=pl.ANY)] + vmem(2),
        out_specs=tuple(vmem(4)),
        scratch_shapes=[pltpu.VMEM((2, 2, C, 576), BF16), pltpu.SemaphoreType.DMA((2,))],
        name="weights",
    )(embed_w.T, block_w, readout, amp_cot)
    weights = [pltpu.with_memory_space_constraint(value, pltpu.VMEM) for value in weights]
    payload = pl.pallas_call(
        states_kernel,
        out_shape=pltpu.VMEM((32 * CHUNK, LY), F32),
        in_specs=vmem(5),
        out_specs=pl.BlockSpec(memory_space=pltpu.VMEM),
        scratch_shapes=[
            pltpu.VMEM((3, 32, LY), F32),
            pltpu.VMEM((24, SITES), BF16),
            pltpu.VMEM((C, SITES), F32),
            pltpu.VMEM((192, SITES), BF16),
            pltpu.VMEM(pair, BF16),
            pltpu.VMEM(pair, BF16),
            pltpu.VMEM(pair, BF16),
            pltpu.VMEM((2, C, SITES), F32),
            pltpu.VMEM((2, C, SITES), F32),
            pltpu.VMEM(pair, F32),
            pltpu.VMEM(pair, F32),
            pltpu.VMEM((2 * C, SITES), BF16),
        ],
        name="states",
    )(fields, *weights)
    parts = lax.all_to_all(payload.reshape(32, CHUNK, LY), ("z", "x"), 0, 0, tiled=True)
    own_sum = jnp.sum(parts, axis=0)
    turned = lax.ppermute(own_sum, ("yh", "z", "x", "yl", "core"), turn_pairs())
    row = lax.broadcasted_iota(jnp.int32, (CHUNK, LY), 0)
    own_sum, row = lax.optimization_barrier((own_sum, row))
    mixed = jnp.where(row < HEAD, own_sum, turned)
    gathered = lax.all_to_all(
        jnp.broadcast_to(mixed, (8, CHUNK, LY)), ("yl", "core"), 0, 0, tiled=True
    )
    gathered = pltpu.with_memory_space_constraint(gathered, pltpu.VMEM)
    log_amp, block_grad, embed_grad = pl.pallas_call(
        final_kernel,
        out_shape=(
            jax.ShapeDtypeStruct((16, C), F32),
            jax.ShapeDtypeStruct((16, 1, 2, 576), F32),
            jax.ShapeDtypeStruct((9, C), F32),
        ),
        in_specs=vmem(1),
        out_specs=tuple(vmem(3)),
        name="outputs",
    )(gathered)
    return log_amp, block_grad, embed_grad.T


def solution(mesh):
    fine = Mesh(mesh.devices.reshape(2, 8, 4, 4, 2), ("yh", "z", "x", "yl", "core"))
    return jax.shard_map(
        local,
        mesh=fine,
        in_specs=(P(("yh", "z", "x"), ("yl", "core"), None), P(), P(), P(), P()),
        out_specs=(P(), P(("yh", "z", "x"), None, None, None), P()),
        check_vma=False,
    )
```
